32 devices in a mesh: section: 4 (over y, x), tok: 4 (over z), head: 2 (over core).
Axes of the slice: x: 2, y: 2, z: 4, core: 2. Of those that a mesh axis runs over, the one named last changes fastest.
Arguments:
- group_in: bfloat16 [4, 512, 2048], P('section', 'tok'), may hold values from -6 to 6
- w_qkv: bfloat16 [4, 3, 2048, 2048], P('section', None, 'tok', 'head'), may hold values from -0.125 to 0.125
- w_out: bfloat16 [4, 2048, 2048], P('section', 'head', 'tok'), may hold values from -0.125 to 0.125
- step_sizes: float32 [4, 512, 4], P('section', 'tok', 'head'), may hold values from 0.05 to 1
- fast_weights: bfloat16 [4, 4, 3, 512, 512], P('section', 'head'), may hold values from -0.25 to 0.25
- momentum: bfloat16 [4, 4, 3, 512, 512], P('section', 'head'), may hold values from -16 to 16
- momentum_decay: float32 [4, 4], P('section', 'head'), may hold values from 0.5 to 0.95
- fast_rate: float32 [4, 4], P('section', 'head'), may hold values from 0.3 to 1
Outputs:
- handed: bfloat16 [4, 512, 2048], P('section', 'tok', 'head')
- fast_next: bfloat16 [4, 4, 3, 512, 512], P('section', 'head')
The draws below stay inside these ranges and needn't reach their ends.
All inputs are finite; a program needn't handle non-finite values.
Results may differ from the reference program's by a relative error of at most 0.015.
Values may be sent and summed in bfloat16 or wider, within the bound.
A program may use at most 128 MiB of HBM per device.

```python
import math
import jax
import jax.numpy as jnp
from jax import lax

D = 2048
HEADS = 4
FIN = 512
FH = 512
NS_ITERS = 2
SECTIONS = 4
GROUP = 512


def level_of(rng, dims, pieces, smallest, largest):
    loudness = 1.0
    for position, parts in pieces:
        draws = jax.random.uniform(jax.random.fold_in(jax.random.fold_in(rng, 6), position), (parts,), jnp.float32, smallest / len(pieces), largest / len(pieces))
        loudness = loudness * jnp.repeat(jnp.exp(draws), dims[position] // parts).reshape((-1,) + (1,) * (len(dims) - 1 - position))
    return loudness


def normal_values(own_key, dims, width, bound, pieces=(), held_as=jnp.bfloat16):
    result = jax.random.normal(own_key, dims, jnp.float32) * width
    if len(pieces) > 0:
        result = level_of(own_key, dims, pieces, -0.22, 0.18) * result
    return jnp.clip(result, min=-bound, max=bound).astype(held_as)


def setup_inputs(seed: int = 0) -> dict:
    streams_of = jax.random.split(jax.random.key(seed), 9)
    return {
        "group_in": normal_values(streams_of[0], (SECTIONS, GROUP, D), 1.0, 6.0, ((0, 4), (1, 4))),
        "w_qkv": normal_values(streams_of[1], (SECTIONS, 3, D, D), D ** -0.5, 0.125, ((0, 4), (2, 4), (3, 2))),
        "w_out": normal_values(streams_of[2], (SECTIONS, D, D), D ** -0.5, 0.125, ((0, 4), (1, 2), (2, 4))),
        "step_sizes": jnp.clip(jnp.exp(math.log(1.0) - 2.9957323 * jax.random.uniform(streams_of[3], (SECTIONS, GROUP, HEADS), jnp.float32) ** level_of(streams_of[3], (SECTIONS, GROUP, HEADS), ((0, 4), (1, 4), (2, 2)), -0.2, 0.2)), 0.05, 1.0),
        "fast_weights": normal_values(streams_of[4], (SECTIONS, HEADS, 3, FIN, FH), FIN ** -0.5, 0.25, ((0, 4), (1, 2))),
        "momentum": normal_values(streams_of[5], (SECTIONS, HEADS, 3, FIN, FH), (GROUP ** 0.5 * 0.125), 16.0, ((0, 4), (1, 2))),
        "momentum_decay": jnp.clip(0.5 + 0.45 * jax.random.uniform(streams_of[6], (SECTIONS, HEADS), jnp.float32) ** level_of(streams_of[6], (SECTIONS, HEADS), ((0, 4), (1, 2)), -0.2, 0.2), 0.5, 0.95),
        "fast_rate": jnp.clip(jnp.exp(math.log(1.0) - 1.2039728 * jax.random.uniform(streams_of[7], (SECTIONS, HEADS), jnp.float32) ** level_of(streams_of[7], (SECTIONS, HEADS), ((0, 4), (1, 2)), -0.2, 0.2)), 0.3, 1.0),
    }


coef_linear = 3.4445
coef_cubic = -4.775
coef_quintic = 2.0315

def rms_rows(values_in, epsilon):
    return values_in * lax.rsqrt(lax.optimization_barrier(jnp.mean(values_in * values_in, axis=-1, keepdims=True)) + epsilon)

def fast_grads(key_rows, value_rows, step_rates, weights):
    key_wide = key_rows.astype(jnp.float32)
    weight_wide = weights.astype(jnp.float32)
    gate_pre = jnp.einsum('thi,hij->thj', key_wide, weight_wide[:, 0])
    up_pre = jnp.einsum('thi,hij->thj', key_wide, weight_wide[:, 1])
    squash = jax.nn.sigmoid(gate_pre)
    hidden = (gate_pre * squash * up_pre).astype(jnp.bfloat16)
    errors = (-(step_rates[:, :, None] * value_rows.astype(jnp.float32))).astype(jnp.bfloat16)
    errors_wide = errors.astype(jnp.float32)
    back_hidden = jnp.einsum('thi,hij->thj', errors_wide, weight_wide[:, 2])
    grad_gate = (back_hidden * up_pre * squash * (1.0 + gate_pre * (1.0 - squash))).astype(jnp.bfloat16)
    grad_up = (back_hidden * gate_pre * squash).astype(jnp.bfloat16)
    grad_first = jnp.einsum('thi,thj->hij', key_wide, grad_gate.astype(jnp.float32))
    grad_third = jnp.einsum('thi,thj->hij', key_wide, grad_up.astype(jnp.float32))
    grad_second = jnp.einsum('thi,thj->hij', errors_wide, hidden.astype(jnp.float32))
    return jnp.stack([grad_first, grad_third, grad_second], axis=1)

def newton_step(iterate):
    iterate_wide = iterate.astype(jnp.float32)
    gram_matrix = jnp.einsum('mij,mik->mjk', iterate_wide, iterate_wide).astype(jnp.bfloat16)
    gram_wide = gram_matrix.astype(jnp.float32)
    cubic_term = jnp.einsum('mij,mjk->mik', iterate_wide, gram_wide)
    rounded = lax.optimization_barrier(cubic_term.astype(jnp.bfloat16))
    quintic_term = jnp.einsum('mij,mjk->mik', rounded.astype(jnp.float32), gram_wide)
    return (coef_linear * iterate_wide + coef_cubic * cubic_term + coef_quintic * quintic_term).astype(jnp.bfloat16)

def apply_fast(queries, updated):
    query_wide = queries.astype(jnp.float32)
    weight_wide = updated.astype(jnp.float32)
    gate_pre = jnp.einsum('thi,hij->thj', query_wide, weight_wide[:, 0])
    up_pre = jnp.einsum('thi,hij->thj', query_wide, weight_wide[:, 1])
    hidden = (jax.nn.silu(gate_pre) * up_pre).astype(jnp.bfloat16)
    output = jnp.einsum('thj,hij->thi', hidden.astype(jnp.float32), weight_wide[:, 2])
    return rms_rows(output, 1e-05).astype(jnp.bfloat16).reshape(GROUP, HEADS * FIN)

def reference(group_in, w_qkv, w_out, step_sizes, fast_weights, momentum, momentum_decay, fast_rate):
    outs_list = []
    weights_list = []
    for level_index in range(SECTIONS):
        tokens = group_in[level_index]
        projected = [jnp.dot(tokens, w_qkv[level_index, component], preferred_element_type=jnp.float32) for component in range(3)]
        queries = rms_rows(projected[0].reshape(GROUP, HEADS, FIN), 1e-06).astype(jnp.bfloat16)
        key_rows = rms_rows(projected[1].reshape(GROUP, HEADS, FIN), 1e-06).astype(jnp.bfloat16)
        value_rows = projected[2].reshape(GROUP, HEADS, FIN).astype(jnp.bfloat16)
        gradients = fast_grads(key_rows, value_rows, step_sizes[level_index], fast_weights[level_index])
        moment = momentum_decay[level_index][:, None, None, None] * momentum[level_index].astype(jnp.float32) + gradients
        norm_values = jnp.sqrt(lax.optimization_barrier(jnp.sum(moment * moment, axis=(2, 3), keepdims=True)))
        iterate = (moment / (norm_values + 1e-06)).astype(jnp.bfloat16).reshape(HEADS * 3, FIN, FH)
        for number in range(NS_ITERS):
            iterate = newton_step(iterate)
        iterate = iterate.reshape(HEADS, 3, FIN, FH)
        updated = (fast_weights[level_index].astype(jnp.float32) - fast_rate[level_index][:, None, None, None] * iterate.astype(jnp.float32)).astype(jnp.bfloat16)
        mixed_heads = apply_fast(queries, updated)
        layer_out = (tokens.astype(jnp.float32) + jnp.dot(mixed_heads, w_out[level_index], preferred_element_type=jnp.float32)).astype(jnp.bfloat16)
        outs_list.append(layer_out)
        weights_list.append(updated)
    stacked = jnp.stack(outs_list)
    handed = jnp.roll(stacked, 1, axis=0)
    return (handed, jnp.stack(weights_list))
```

```python
import jax
import jax.numpy as jnp
from jax import lax
from jax.sharding import PartitionSpec as P

NS_ITERS = 2


coef_linear = 3.4445
coef_cubic = -4.775
coef_quintic = 2.0315


def passed_along(value, axis, steps):
    count = lax.axis_size(axis)
    pairs = [(source, (source + steps) % count) for source in range(count)]
    return lax.ppermute(value, axis, pairs)


def rms_rows(values_in, epsilon):
    return values_in * lax.rsqrt(jnp.mean(values_in * values_in, axis=-1, keepdims=True) + epsilon)


def fast_grads(key_rows, value_rows, step_rates, weights):
    gate_pre = jnp.einsum(
        "thi,hij->thj", key_rows, weights[:, 0], preferred_element_type=jnp.float32
    )
    up_pre = jnp.einsum("thi,hij->thj", key_rows, weights[:, 1], preferred_element_type=jnp.float32)
    squash = jax.nn.sigmoid(gate_pre)
    hidden = (gate_pre * squash * up_pre).astype(jnp.bfloat16)
    errors = (-(step_rates[:, :, None] * value_rows.astype(jnp.float32))).astype(jnp.bfloat16)
    back_hidden = jnp.einsum(
        "thi,hij->thj", errors, weights[:, 2], preferred_element_type=jnp.float32
    )
    grad_gate = (back_hidden * up_pre * squash * (1.0 + gate_pre * (1.0 - squash))).astype(
        jnp.bfloat16
    )
    grad_up = (back_hidden * gate_pre * squash).astype(jnp.bfloat16)
    grad_first = jnp.einsum("thi,thj->hij", key_rows, grad_gate, preferred_element_type=jnp.float32)
    grad_third = jnp.einsum("thi,thj->hij", key_rows, grad_up, preferred_element_type=jnp.float32)
    grad_second = jnp.einsum("thi,thj->hij", errors, hidden, preferred_element_type=jnp.float32)
    return jnp.stack([grad_first, grad_third, grad_second], axis=1)


def newton_step(rows_in, gathered):
    gram_matrix = jnp.einsum(
        "mij,mik->mjk", gathered, gathered, preferred_element_type=jnp.float32
    ).astype(jnp.bfloat16)
    cubic_term = jnp.einsum(
        "mij,mjk->mik", rows_in, gram_matrix, preferred_element_type=jnp.float32
    )
    quintic_term = jnp.einsum(
        "mij,mjk->mik",
        cubic_term.astype(jnp.bfloat16),
        gram_matrix,
        preferred_element_type=jnp.float32,
    )
    return (
        coef_linear * rows_in.astype(jnp.float32)
        + coef_cubic * cubic_term
        + coef_quintic * quintic_term
    ).astype(jnp.bfloat16)


def apply_fast(queries, updated):
    gate_pre = jnp.einsum(
        "thi,hij->thj", queries, updated[:, 0], preferred_element_type=jnp.float32
    )
    up_pre = jnp.einsum("thi,hij->thj", queries, updated[:, 1], preferred_element_type=jnp.float32)
    hidden = (jax.nn.silu(gate_pre) * up_pre).astype(jnp.bfloat16)
    output = jnp.einsum("thj,hij->thi", hidden, updated[:, 2], preferred_element_type=jnp.float32)
    return rms_rows(output, 1e-05).astype(jnp.bfloat16)


def shards(group_in, w_qkv, w_out, step_sizes, fast_weights, momentum, momentum_decay, fast_rate):
    tokens = group_in[0]
    tok_rows = tokens.shape[0]
    local_heads = fast_weights.shape[1]
    fan_width = fast_weights.shape[3]
    hid_width = fast_weights.shape[4]
    half_width = w_qkv.shape[3]
    columns = lax.all_to_all(tokens, "tok", split_axis=1, concat_axis=0, tiled=True)
    all_rows = columns.shape[0]
    rates = lax.all_gather(step_sizes[0], "tok", axis=0, tiled=True)
    partial_kv = jnp.einsum(
        "td,jde->jte", columns, w_qkv[0, 1:], preferred_element_type=jnp.float32
    ).astype(jnp.bfloat16)
    partial_q = jnp.dot(columns, w_qkv[0, 0], preferred_element_type=jnp.float32).astype(
        jnp.bfloat16
    )
    summed_kv = lax.psum(partial_kv, "tok").astype(jnp.float32)
    summed_q = lax.psum(partial_q, "tok").astype(jnp.float32)
    shaped = summed_kv.reshape(2, all_rows, local_heads, fan_width)
    key_rows = rms_rows(shaped[0], 1e-06).astype(jnp.bfloat16)
    value_rows = shaped[1].astype(jnp.bfloat16)
    queries = rms_rows(summed_q.reshape(all_rows, local_heads, fan_width), 1e-06).astype(
        jnp.bfloat16
    )
    summed = fast_grads(key_rows, value_rows, rates, fast_weights[0])
    decay_rate = momentum_decay[0][:, None, None, None]
    moment = decay_rate * momentum[0].astype(jnp.float32) + summed
    norm_values = jnp.sqrt(jnp.sum(moment * moment, axis=(2, 3), keepdims=True))
    iterate = (moment / (norm_values + 1e-06)).astype(jnp.bfloat16)
    iterate = iterate.reshape(local_heads * 3, fan_width, hid_width)
    for number in range(NS_ITERS):
        iterate = newton_step(iterate, iterate)
    iterate = iterate.reshape(local_heads, 3, fan_width, hid_width)
    updated = (
        fast_weights[0].astype(jnp.float32)
        - fast_rate[0][:, None, None, None] * iterate.astype(jnp.float32)
    ).astype(jnp.bfloat16)
    mixed_heads = apply_fast(queries, updated).reshape(all_rows, half_width)
    partial_out = jnp.dot(mixed_heads, w_out[0], preferred_element_type=jnp.float32)
    own_rows = lax.all_to_all(
        partial_out.astype(jnp.bfloat16), "tok", split_axis=0, concat_axis=1, tiled=True
    )
    summed_out = lax.psum_scatter(own_rows, "head", scatter_dimension=1, tiled=True).astype(
        jnp.float32
    )
    share_width = summed_out.shape[1]
    own_tokens = lax.dynamic_slice_in_dim(
        tokens, lax.axis_index("head") * share_width, share_width, 1
    )
    layer_out = (own_tokens.astype(jnp.float32) + summed_out).astype(jnp.bfloat16)
    handed = passed_along(layer_out[None], "section", 1)
    return (handed, updated[None])


def solution(mesh):
    placed = (
        P("section", "tok", None),
        P("section", None, "tok", "head"),
        P("section", "head", "tok"),
        P("section", "tok", "head"),
        P("section", "head", None, None, None),
        P("section", "head", None, None, None),
        P("section", "head"),
        P("section", "head"),
    )
    return jax.shard_map(
        shards,
        mesh=mesh,
        in_specs=placed,
        out_specs=(P("section", "tok", "head"), P("section", "head", None, None, None)),
        check_vma=False,
    )
```

```python
import functools

import jax
import jax.numpy as jnp
from jax import lax
from jax.experimental import pallas as pl
from jax.experimental.pallas import tpu as pltpu
from jax.sharding import PartitionSpec as P

NS_ITERS = 2


coef_linear = 3.4445
coef_cubic = -4.775
coef_quintic = 2.0315


def passed_along(value, axis, steps):
    count = lax.axis_size(axis)
    pairs = [(source, (source + steps) % count) for source in range(count)]
    return lax.ppermute(value, axis, pairs)


def rms_rows(values_in, epsilon):
    return values_in * lax.rsqrt(jnp.mean(values_in * values_in, axis=-1, keepdims=True) + epsilon)


def fast_grads(key_rows, value_rows, step_rates, weights):
    gate_pre = jnp.einsum(
        "thi,hij->thj", key_rows, weights[:, 0], preferred_element_type=jnp.float32
    )
    up_pre = jnp.einsum("thi,hij->thj", key_rows, weights[:, 1], preferred_element_type=jnp.float32)
    squash = jax.nn.sigmoid(gate_pre)
    hidden = (gate_pre * squash * up_pre).astype(jnp.bfloat16)
    errors = (-(step_rates[:, :, None] * value_rows.astype(jnp.float32))).astype(jnp.bfloat16)
    back_hidden = jnp.einsum(
        "thi,hij->thj", errors, weights[:, 2], preferred_element_type=jnp.float32
    )
    grad_gate = (back_hidden * up_pre * squash * (1.0 + gate_pre * (1.0 - squash))).astype(
        jnp.bfloat16
    )
    grad_up = (back_hidden * gate_pre * squash).astype(jnp.bfloat16)
    grad_first = jnp.einsum("thi,thj->hij", key_rows, grad_gate, preferred_element_type=jnp.float32)
    grad_third = jnp.einsum("thi,thj->hij", key_rows, grad_up, preferred_element_type=jnp.float32)
    grad_second = jnp.einsum("thi,thj->hij", errors, hidden, preferred_element_type=jnp.float32)
    return jnp.stack([grad_first, grad_third, grad_second], axis=1)


def newton_step(rows_in, gathered):
    gram_matrix = jnp.einsum(
        "mij,mik->mjk", gathered, gathered, preferred_element_type=jnp.float32
    ).astype(jnp.bfloat16)
    cubic_term = jnp.einsum(
        "mij,mjk->mik", rows_in, gram_matrix, preferred_element_type=jnp.float32
    )
    quintic_term = jnp.einsum(
        "mij,mjk->mik",
        cubic_term.astype(jnp.bfloat16),
        gram_matrix,
        preferred_element_type=jnp.float32,
    )
    return (
        coef_linear * rows_in.astype(jnp.float32)
        + coef_cubic * cubic_term
        + coef_quintic * quintic_term
    ).astype(jnp.bfloat16)


def apply_fast(queries, updated):
    gate_pre = jnp.einsum(
        "thi,hij->thj", queries, updated[:, 0], preferred_element_type=jnp.float32
    )
    up_pre = jnp.einsum("thi,hij->thj", queries, updated[:, 1], preferred_element_type=jnp.float32)
    hidden = (jax.nn.silu(gate_pre) * up_pre).astype(jnp.bfloat16)
    output = jnp.einsum("thj,hij->thi", hidden, updated[:, 2], preferred_element_type=jnp.float32)
    return rms_rows(output, 1e-05).astype(jnp.bfloat16)


def plain_shards(group_in, w_qkv, w_out, step_sizes, fast_weights, momentum, momentum_decay, fast_rate):
    tokens = group_in[0]
    tok_rows = tokens.shape[0]
    local_heads = fast_weights.shape[1]
    fan_width = fast_weights.shape[3]
    hid_width = fast_weights.shape[4]
    half_width = w_qkv.shape[3]
    columns = lax.all_to_all(tokens, "tok", split_axis=1, concat_axis=0, tiled=True)
    all_rows = columns.shape[0]
    rates = lax.all_gather(step_sizes[0], "tok", axis=0, tiled=True)
    partial_kv = jnp.einsum(
        "td,jde->jte", columns, w_qkv[0, 1:], preferred_element_type=jnp.float32
    ).astype(jnp.bfloat16)
    partial_q = jnp.dot(columns, w_qkv[0, 0], preferred_element_type=jnp.float32).astype(
        jnp.bfloat16
    )
    summed_kv = lax.psum(partial_kv, "tok").astype(jnp.float32)
    summed_q = lax.psum(partial_q, "tok").astype(jnp.float32)
    shaped = summed_kv.reshape(2, all_rows, local_heads, fan_width)
    key_rows = rms_rows(shaped[0], 1e-06).astype(jnp.bfloat16)
    value_rows = shaped[1].astype(jnp.bfloat16)
    queries = rms_rows(summed_q.reshape(all_rows, local_heads, fan_width), 1e-06).astype(
        jnp.bfloat16
    )
    summed = fast_grads(key_rows, value_rows, rates, fast_weights[0])
    decay_rate = momentum_decay[0][:, None, None, None]
    moment = decay_rate * momentum[0].astype(jnp.float32) + summed
    norm_values = jnp.sqrt(jnp.sum(moment * moment, axis=(2, 3), keepdims=True))
    iterate = (moment / (norm_values + 1e-06)).astype(jnp.bfloat16)
    iterate = iterate.reshape(local_heads * 3, fan_width, hid_width)
    for number in range(NS_ITERS):
        iterate = newton_step(iterate, iterate)
    iterate = iterate.reshape(local_heads, 3, fan_width, hid_width)
    updated = (
        fast_weights[0].astype(jnp.float32)
        - fast_rate[0][:, None, None, None] * iterate.astype(jnp.float32)
    ).astype(jnp.bfloat16)
    mixed_heads = apply_fast(queries, updated).reshape(all_rows, half_width)
    partial_out = jnp.dot(mixed_heads, w_out[0], preferred_element_type=jnp.float32)
    own_rows = lax.all_to_all(
        partial_out.astype(jnp.bfloat16), "tok", split_axis=0, concat_axis=1, tiled=True
    )
    summed_out = lax.psum_scatter(own_rows, "head", scatter_dimension=1, tiled=True).astype(
        jnp.float32
    )
    share_width = summed_out.shape[1]
    own_tokens = lax.dynamic_slice_in_dim(
        tokens, lax.axis_index("head") * share_width, share_width, 1
    )
    layer_out = (own_tokens.astype(jnp.float32) + summed_out).astype(jnp.bfloat16)
    handed = passed_along(layer_out[None], "section", 1)
    return (handed, updated[None])


MESH = pl.DeviceIdType.MESH
F32 = jnp.float32
BF16 = jnp.bfloat16
CHUNK = 32
QUERY_CHUNK = 64


def dot(a, b, a_dim=1, b_dim=0):
    return lax.dot_general(a, b, (((a_dim,), (b_dim,)), ((), ())), preferred_element_type=F32)


def layer_kernel(
    dims, x_ref, rate_ref, decay_ref, fast_rate_ref, wqkv_hbm, wout_hbm, fast_hbm, mom_hbm,
    handed_ref, next_hbm,
    wqkv, wout, fast, mom, moved, columns, rates, rate_in, part, outer_in, cross_in, final,
    qpart, qouter_in, qcross_in, qfinal, grad, updated, mixed, half_out, half_in, sent, hand,
    load_sem, x_send, x_recv, fwd_send, fwd_recv, rate_send, rate_recv,
    s_send, o_recv, c_recv, f_send, f_recv, qs_send, qo_recv, qc_recv, qf_send, qf_recv,
    next_sem, half_send, half_recv, hand_send, hand_recv,
):
    sections, n, heads, fin, hid = dims
    rows = x_ref.shape[0]
    width = columns.shape[3]
    half = rows // 2
    all_rows = rows * n
    local = heads * fin
    per_block = rows // CHUNK
    chunks = n * per_block
    qchunks = all_rows // QUERY_CHUNK
    sec, me, core = lax.axis_index("section"), lax.axis_index("tok"), lax.axis_index("head")
    mate = 1 - core
    right = me // (n // 2)
    inner, outer = me + 1 - 2 * right, me - 1 + 2 * right
    is_end = (me == 0) | (me == n - 1)
    is_mid = (me == n // 2 - 1) | (me == n // 2)
    share = n // 2
    next_sec, last_sec = lax.rem(sec + 1, sections), lax.rem(sec + sections - 1, sections)
    peers = [lax.rem(me + step, n) for step in range(1, n)]

    loads = [
        pltpu.make_async_copy(src, dst, load_sem.at[i])
        for i, (src, dst) in enumerate(
            [(wqkv_hbm, wqkv), (fast_hbm, fast), (mom_hbm, mom), (wout_hbm, wout)]
        )
    ]
    for load in loads:
        load.start()

    barrier = pltpu.get_barrier_semaphore()

    def greet(device):
        pl.semaphore_signal(barrier, inc=1, device_id=device, device_id_type=MESH)

    for peer in peers:
        greet((sec, peer, core))
    greet((sec, me, mate))
    for j in range(share):
        greet((next_sec, core * share + j, me // share))
        greet((last_sec, core * share + j, me // share))
    pl.semaphore_wait(barrier, n + 2 * share)

    def remote(src, dst, send, recv, device):
        return pltpu.make_async_remote_copy(
            src_ref=src, dst_ref=dst, send_sem=send, recv_sem=recv,
            device_id=device, device_id_type=MESH,
        )

    def x_copy(peer):
        start = pl.multiple_of(peer * width, 128)
        return remote(
            x_ref.at[pl.ds(core * half, half), pl.ds(start, width)], columns.at[me, core],
            x_send.at[peer], x_recv.at[me], (sec, peer, core),
        )

    def x_from(source):
        return remote(
            columns.at[source, core], columns.at[source, core],
            x_send.at[source], x_recv.at[source], (sec, source, core),
        )

    def x_forward(source):
        return remote(
            columns.at[source, core], columns.at[source, core],
            fwd_send.at[source], fwd_recv.at[source], (sec, me, mate),
        )

    def x_forwarded(source):
        return remote(
            columns.at[source, mate], columns.at[source, mate],
            fwd_send.at[source], fwd_recv.at[source], (sec, me, mate),
        )

    def rate_copy(peer, slot):
        return remote(
            rate_ref, rate_in.at[slot], rate_send.at[peer], rate_recv.at[slot], (sec, peer, core)
        )

    for peer in peers:
        x_copy(peer).start()
        rate_copy(peer, me).start()
    own = x_ref[:, pl.ds(pl.multiple_of(me * width, 128), width)]
    columns[me] = own.reshape(2, half, width)

    def normed(values, epsilon):
        return values * lax.rsqrt(jnp.mean(values * values, axis=-1, keepdims=True) + epsilon)

    def stages(part, outer_in, cross_in, final, s_send, o_recv, c_recv, f_send, f_recv, finish):
        def to_outer_in(c):
            return remote(part.at[c], outer_in.at[c], s_send.at[c], o_recv.at[c], (sec, inner, core))

        def to_cross_in(c):
            return remote(part.at[c], cross_in.at[c], s_send.at[c], c_recv.at[c], (sec, inner, core))

        def outward(c):
            return remote(final.at[c], final.at[c], f_send.at[c], f_recv.at[c], (sec, outer, core))

        def gather(c):
            @pl.when(jnp.logical_not(is_end))
            def _():
                to_outer_in(c).wait_recv()
                part[c] = (part[c].astype(F32) + outer_in[c].astype(F32)).astype(BF16)

            @pl.when(is_mid)
            def _():
                to_cross_in(c).start()

            @pl.when(jnp.logical_not(is_mid))
            def _():
                to_outer_in(c).start()

        def spread(c):
            @pl.when(is_mid)
            def _():
                to_cross_in(c).wait_recv()
                finish(c, part[c].astype(F32) + cross_in[c].astype(F32))

            @pl.when(jnp.logical_not(is_mid))
            def _():
                outward(c).wait_recv()

            @pl.when(jnp.logical_not(is_end))
            def _():
                outward(c).start()

        def drain(c):
            to_outer_in(c).wait_send()

            @pl.when(jnp.logical_not(is_end))
            def _():
                outward(c).wait_send()

        return gather, spread, drain

    def finish_kv(c, total):
        block, row = c // per_block, (c % per_block) * CHUNK
        for h in range(heads):
            lanes = slice(h * fin, (h + 1) * fin)
            final[c, :, lanes] = normed(total[:, lanes], 1e-06).astype(BF16)
            value = total[:, local + h * fin : local + (h + 1) * fin].astype(BF16).astype(F32)
            rate = rates[h, block, pl.ds(pl.multiple_of(row, CHUNK), CHUNK), :][:, :1]
            final[c, :, local + h * fin : local + (h + 1) * fin] = (-(rate * value)).astype(BF16)

    def finish_q(c, total):
        for h in range(heads):
            lanes = slice(h * fin, (h + 1) * fin)
            qfinal[c, :, lanes] = normed(total[:, lanes], 1e-06).astype(BF16)

    gather, spread, drain = stages(
        part, outer_in, cross_in, final, s_send, o_recv, c_recv, f_send, f_recv, finish_kv
    )
    qgather, qspread, qdrain = stages(
        qpart, qouter_in, qcross_in, qfinal, qs_send, qo_recv, qc_recv, qf_send, qf_recv, finish_q
    )

    for block in range(n):
        @pl.when(me != block)
        def _():
            x_from(block).wait_recv()
            x_forward(block).start()
            rate_copy(block, block).wait_recv()
            x_forwarded(block).wait_recv()
            for h in range(heads):
                line = rate_in[block, h : h + 1, :]
                rates[h, block] = jnp.transpose(jnp.broadcast_to(line, (rows, rows)))

        @pl.when(me == block)
        def _():
            for h in range(heads):
                line = rate_ref[h : h + 1, :]
                rates[h, block] = jnp.transpose(jnp.broadcast_to(line, (rows, rows)))

        if block == 0:
            loads[0].wait()
        tile = columns[block].reshape(rows, width)
        for j in range(2):
            made = dot(tile, wqkv[j + 1]).astype(BF16).reshape(per_block, CHUNK, local)
            part[block * per_block : (block + 1) * per_block, :, j * local : (j + 1) * local] = made

        @pl.loop(block * per_block, (block + 1) * per_block)
        def _(c):
            gather(c)

            @pl.when(c >= 2)
            def _():
                spread(c - 2)

    tile = columns[...].reshape(all_rows, width)
    qpart[...] = dot(tile, wqkv[0]).astype(BF16).reshape(qchunks, QUERY_CHUNK, local)

    @pl.when(is_end)
    def _():
        @pl.loop(0, qchunks)
        def _(c):
            qgather(c)

    spread(chunks - 2)
    spread(chunks - 1)

    def query_step(c):
        @pl.when(jnp.logical_not(is_end) & (c < qchunks))
        def _():
            qgather(c)

        @pl.when(jnp.logical_not(is_end) & (c >= 2) & (c < qchunks + 2))
        def _():
            qspread(c - 2)

    loads[1].wait()
    loads[2].wait()

    def store_next(m):
        return pltpu.make_async_copy(updated.at[m], next_hbm.at[m], next_sem.at[m])

    @pl.loop(0, heads)
    def _(h):
        lanes = pl.ds(pl.multiple_of(h * fin, 128), fin)
        err_lanes = pl.ds(pl.multiple_of(local + h * fin, 128), fin)
        keys = final[:, :, lanes].reshape(all_rows, fin)
        errors = final[:, :, err_lanes].reshape(all_rows, fin)
        gate = dot(keys, fast[h * 3])
        squash = jax.nn.sigmoid(gate)
        up = dot(keys, fast[h * 3 + 1])
        hidden = (gate * squash * up).astype(BF16)
        back = dot(errors, fast[h * 3 + 2])
        grad_gate = (back * up * squash * (1.0 + gate * (1.0 - squash))).astype(BF16)
        grad_up = (back * gate * squash).astype(BF16)
        grad[0] = dot(keys, grad_gate, 0, 0)
        grad[1] = dot(keys, grad_up, 0, 0)
        grad[2] = dot(errors, hidden, 0, 0)

        @pl.loop(0, 3)
        def _(j):
            m = h * 3 + j
            moment = decay_ref[h] * mom[m].astype(F32) + grad[j]
            size = jnp.sqrt(jnp.sum(moment * moment))
            moved[...] = (moment / (size + 1e-06)).astype(BF16)
            for _ in range(NS_ITERS):
                it = moved[...]
                gram = dot(it, it, 0, 0).astype(BF16)
                cubic = dot(it, gram)
                quintic = dot(cubic.astype(BF16), gram)
                moved[...] = (
                    coef_linear * it.astype(F32) + coef_cubic * cubic + coef_quintic * quintic
                ).astype(BF16)
            updated[m] = (
                fast[m].astype(F32) - fast_rate_ref[h] * moved[...].astype(F32)
            ).astype(BF16)
            store_next(m).start()
            query_step(m)

    @pl.loop(heads * 3, qchunks + 2)
    def _(c):
        query_step(c)

    @pl.when(is_end)
    def _():
        @pl.loop(0, qchunks)
        def _(c):
            qspread(c)

    @pl.loop(0, heads)
    def _(h):
        lanes = pl.ds(pl.multiple_of(h * fin, 128), fin)
        queries = qfinal[:, :, lanes].reshape(all_rows, fin)
        gate = dot(queries, updated[h * 3])
        up = dot(queries, updated[h * 3 + 1])
        hidden = (gate * jax.nn.sigmoid(gate) * up).astype(BF16)
        output = dot(hidden, updated[h * 3 + 2], 1, 1)
        mixed[:, lanes] = normed(output, 1e-05).astype(BF16)

    loads[3].wait()
    span = all_rows // 2
    mine = pl.ds(pl.multiple_of(core * span, 128), span)
    theirs = pl.ds(pl.multiple_of(mate * span, 128), span)
    half_out[...] = dot(mixed[theirs, :], wout[...]).astype(BF16)
    swap = remote(half_out, half_in, half_send, half_recv, (sec, me, mate))
    swap.start()
    summed = dot(mixed[mine, :], wout[...])
    residual = columns[pl.ds(core * share, share)].reshape(span, width).astype(F32)
    swap.wait()
    sent[...] = (residual + (summed + half_in[...].astype(F32))).astype(BF16).reshape(
        share, rows, width
    )

    def hand_over(j, slot):
        return remote(
            sent.at[j], hand.at[slot], hand_send.at[j], hand_recv.at[slot],
            (next_sec, core * share + j, me // share),
        )

    for j in range(share):
        hand_over(j, lax.rem(me, share)).start()
    for peer in peers:
        x_copy(peer).wait_send()
        rate_copy(peer, me).wait_send()
        x_forward(peer).wait_send()

    @pl.loop(0, chunks)
    def _(c):
        drain(c)

    @pl.loop(0, qchunks)
    def _(c):
        qdrain(c)

    for m in range(heads * 3):
        store_next(m).wait()
    for j in range(share):
        hand_over(j, j).wait_recv()
        handed_ref[:, j * width : (j + 1) * width] = hand[j]
    for j in range(share):
        hand_over(j, j).wait_send()


def fused_shards(
    group_in, w_qkv, w_out, step_sizes, fast_weights, momentum, momentum_decay, fast_rate
):
    sections, n = lax.axis_size("section"), lax.axis_size("tok")
    tokens = group_in[0]
    rows = tokens.shape[0]
    heads, fin, hid = fast_weights.shape[1], fast_weights.shape[3], fast_weights.shape[4]
    local, width = heads * fin, w_qkv.shape[2]
    all_rows, share = rows * n, n // 2
    chunks, qchunks = all_rows // CHUNK, all_rows // QUERY_CHUNK
    matrices = heads * 3
    rate_lines = jnp.pad(step_sizes[0].T, ((0, 8 - heads), (0, 0)))
    vmem = pl.BlockSpec(memory_space=pltpu.VMEM)
    smem = pl.BlockSpec(memory_space=pltpu.SMEM)
    anywhere = pl.BlockSpec(memory_space=pl.ANY)
    dma = pltpu.SemaphoreType.DMA
    handed, updated = pl.pallas_call(
        functools.partial(layer_kernel, (sections, n, heads, fin, hid)),
        out_shape=(
            jax.ShapeDtypeStruct((rows, share * width), BF16),
            jax.ShapeDtypeStruct((matrices, fin, hid), BF16),
        ),
        in_specs=[vmem, vmem, smem, smem, anywhere, anywhere, anywhere, anywhere],
        out_specs=(vmem, anywhere),
        scratch_shapes=[
            pltpu.VMEM(w_qkv.shape[1:], BF16),
            pltpu.VMEM(w_out.shape[1:], BF16),
            pltpu.VMEM((matrices, fin, hid), BF16),
            pltpu.VMEM((matrices, fin, hid), BF16),
            pltpu.VMEM((fin, hid), BF16),
            pltpu.VMEM((n, 2, rows // 2, width), BF16),
            pltpu.VMEM((heads, n, rows, rows), F32),
            pltpu.VMEM((n, 8, rows), F32),
            pltpu.VMEM((chunks, CHUNK, 2 * local), BF16),
            pltpu.VMEM((chunks, CHUNK, 2 * local), BF16),
            pltpu.VMEM((chunks, CHUNK, 2 * local), BF16),
            pltpu.VMEM((chunks, CHUNK, 2 * local), BF16),
            pltpu.VMEM((qchunks, QUERY_CHUNK, local), BF16),
            pltpu.VMEM((qchunks, QUERY_CHUNK, local), BF16),
            pltpu.VMEM((qchunks, QUERY_CHUNK, local), BF16),
            pltpu.VMEM((qchunks, QUERY_CHUNK, local), BF16),
            pltpu.VMEM((3, fin, hid), F32),
            pltpu.VMEM((matrices, fin, hid), BF16),
            pltpu.VMEM((all_rows, local), BF16),
            pltpu.VMEM((all_rows // 2, width), BF16),
            pltpu.VMEM((all_rows // 2, width), BF16),
            pltpu.VMEM((share, rows, width), BF16),
            pltpu.VMEM((share, rows, width), BF16),
            dma((4,)),
            dma((n,)), dma((n,)), dma((n,)), dma((n,)), dma((n,)), dma((n,)),
            dma((chunks,)), dma((chunks,)), dma((chunks,)), dma((chunks,)), dma((chunks,)),
            dma((qchunks,)), dma((qchunks,)), dma((qchunks,)), dma((qchunks,)), dma((qchunks,)),
            dma((matrices,)), dma(()), dma(()), dma((share,)), dma((share,)),
        ],
        compiler_params=pltpu.CompilerParams(
            collective_id=0, has_side_effects=True, vmem_limit_bytes=60 << 20
        ),
    )(
        tokens, rate_lines, momentum_decay[0], fast_rate[0], w_qkv[0], w_out[0],
        fast_weights[0].reshape(matrices, fin, hid), momentum[0].reshape(matrices, fin, hid),
    )
    return (handed[None], updated.reshape(fast_weights.shape))


def shards(group_in, w_qkv, w_out, *rest):
    n, cores = lax.axis_size("tok"), lax.axis_size("head")
    rows, width, local = group_in.shape[1], w_qkv.shape[2], w_qkv.shape[3]
    held = 2 * (24 * rows * n * local + 12 * rows * n * width + 4 * w_qkv[0].size)
    fits = (
        held < 44 << 20
        and cores == 2
        and n % 2 == 0
        and n >= 4
        and rows == 128
        and width % 128 == 0
        and w_out.shape[2] == width
        and lax.axis_size("section") > 2
    )
    return (fused_shards if fits else plain_shards)(group_in, w_qkv, w_out, *rest)


def solution(mesh):
    placed = (
        P("section", "tok", None),
        P("section", None, "tok", "head"),
        P("section", "head", "tok"),
        P("section", "tok", "head"),
        P("section", "head", None, None, None),
        P("section", "head", None, None, None),
        P("section", "head"),
        P("section", "head"),
    )
    return jax.shard_map(
        shards,
        mesh=mesh,
        in_specs=placed,
        out_specs=(P("section", "tok", "head"), P("section", "head", None, None, None)),
        check_vma=False,
    )
```

```python
import functools

import jax
import jax.numpy as jnp
from jax import lax
from jax.experimental import pallas as pl
from jax.experimental.pallas import tpu as pltpu
from jax.sharding import PartitionSpec as P

NS_ITERS = 2


coef_linear = 3.4445
coef_cubic = -4.775
coef_quintic = 2.0315


def passed_along(value, axis, steps):
    count = lax.axis_size(axis)
    pairs = [(source, (source + steps) % count) for source in range(count)]
    return lax.ppermute(value, axis, pairs)


def rms_rows(values_in, epsilon):
    return values_in * lax.rsqrt(jnp.mean(values_in * values_in, axis=-1, keepdims=True) + epsilon)


def fast_grads(key_rows, value_rows, step_rates, weights):
    gate_pre = jnp.einsum(
        "thi,hij->thj", key_rows, weights[:, 0], preferred_element_type=jnp.float32
    )
    up_pre = jnp.einsum("thi,hij->thj", key_rows, weights[:, 1], preferred_element_type=jnp.float32)
    squash = jax.nn.sigmoid(gate_pre)
    hidden = (gate_pre * squash * up_pre).astype(jnp.bfloat16)
    errors = (-(step_rates[:, :, None] * value_rows.astype(jnp.float32))).astype(jnp.bfloat16)
    back_hidden = jnp.einsum(
        "thi,hij->thj", errors, weights[:, 2], preferred_element_type=jnp.float32
    )
    grad_gate = (back_hidden * up_pre * squash * (1.0 + gate_pre * (1.0 - squash))).astype(
        jnp.bfloat16
    )
    grad_up = (back_hidden * gate_pre * squash).astype(jnp.bfloat16)
    grad_first = jnp.einsum("thi,thj->hij", key_rows, grad_gate, preferred_element_type=jnp.float32)
    grad_third = jnp.einsum("thi,thj->hij", key_rows, grad_up, preferred_element_type=jnp.float32)
    grad_second = jnp.einsum("thi,thj->hij", errors, hidden, preferred_element_type=jnp.float32)
    return jnp.stack([grad_first, grad_third, grad_second], axis=1)


def newton_step(rows_in, gathered):
    gram_matrix = jnp.einsum(
        "mij,mik->mjk", gathered, gathered, preferred_element_type=jnp.float32
    ).astype(jnp.bfloat16)
    cubic_term = jnp.einsum(
        "mij,mjk->mik", rows_in, gram_matrix, preferred_element_type=jnp.float32
    )
    quintic_term = jnp.einsum(
        "mij,mjk->mik",
        cubic_term.astype(jnp.bfloat16),
        gram_matrix,
        preferred_element_type=jnp.float32,
    )
    return (
        coef_linear * rows_in.astype(jnp.float32)
        + coef_cubic * cubic_term
        + coef_quintic * quintic_term
    ).astype(jnp.bfloat16)


def apply_fast(queries, updated):
    gate_pre = jnp.einsum(
        "thi,hij->thj", queries, updated[:, 0], preferred_element_type=jnp.float32
    )
    up_pre = jnp.einsum("thi,hij->thj", queries, updated[:, 1], preferred_element_type=jnp.float32)
    hidden = (jax.nn.silu(gate_pre) * up_pre).astype(jnp.bfloat16)
    output = jnp.einsum("thj,hij->thi", hidden, updated[:, 2], preferred_element_type=jnp.float32)
    return rms_rows(output, 1e-05).astype(jnp.bfloat16)


def plain_shards(group_in, w_qkv, w_out, step_sizes, fast_weights, momentum, momentum_decay, fast_rate):
    tokens = group_in[0]
    tok_rows = tokens.shape[0]
    local_heads = fast_weights.shape[1]
    fan_width = fast_weights.shape[3]
    hid_width = fast_weights.shape[4]
    half_width = w_qkv.shape[3]
    columns = lax.all_to_all(tokens, "tok", split_axis=1, concat_axis=0, tiled=True)
    all_rows = columns.shape[0]
    rates = lax.all_gather(step_sizes[0], "tok", axis=0, tiled=True)
    partial_kv = jnp.einsum(
        "td,jde->jte", columns, w_qkv[0, 1:], preferred_element_type=jnp.float32
    ).astype(jnp.bfloat16)
    partial_q = jnp.dot(columns, w_qkv[0, 0], preferred_element_type=jnp.float32).astype(
        jnp.bfloat16
    )
    summed_kv = lax.psum(partial_kv, "tok").astype(jnp.float32)
    summed_q = lax.psum(partial_q, "tok").astype(jnp.float32)
    shaped = summed_kv.reshape(2, all_rows, local_heads, fan_width)
    key_rows = rms_rows(shaped[0], 1e-06).astype(jnp.bfloat16)
    value_rows = shaped[1].astype(jnp.bfloat16)
    queries = rms_rows(summed_q.reshape(all_rows, local_heads, fan_width), 1e-06).astype(
        jnp.bfloat16
    )
    summed = fast_grads(key_rows, value_rows, rates, fast_weights[0])
    decay_rate = momentum_decay[0][:, None, None, None]
    moment = decay_rate * momentum[0].astype(jnp.float32) + summed
    norm_values = jnp.sqrt(jnp.sum(moment * moment, axis=(2, 3), keepdims=True))
    iterate = (moment / (norm_values + 1e-06)).astype(jnp.bfloat16)
    iterate = iterate.reshape(local_heads * 3, fan_width, hid_width)
    for number in range(NS_ITERS):
        iterate = newton_step(iterate, iterate)
    iterate = iterate.reshape(local_heads, 3, fan_width, hid_width)
    updated = (
        fast_weights[0].astype(jnp.float32)
        - fast_rate[0][:, None, None, None] * iterate.astype(jnp.float32)
    ).astype(jnp.bfloat16)
    mixed_heads = apply_fast(queries, updated).reshape(all_rows, half_width)
    partial_out = jnp.dot(mixed_heads, w_out[0], preferred_element_type=jnp.float32)
    own_rows = lax.all_to_all(
        partial_out.astype(jnp.bfloat16), "tok", split_axis=0, concat_axis=1, tiled=True
    )
    summed_out = lax.psum_scatter(own_rows, "head", scatter_dimension=1, tiled=True).astype(
        jnp.float32
    )
    share_width = summed_out.shape[1]
    own_tokens = lax.dynamic_slice_in_dim(
        tokens, lax.axis_index("head") * share_width, share_width, 1
    )
    layer_out = (own_tokens.astype(jnp.float32) + summed_out).astype(jnp.bfloat16)
    handed = passed_along(layer_out[None], "section", 1)
    return (handed, updated[None])


MESH = pl.DeviceIdType.MESH
F32 = jnp.float32
BF16 = jnp.bfloat16
CHUNK = 32
QUERY_CHUNK = 64
LAG = 3


def dot(a, b, a_dim=1, b_dim=0):
    return lax.dot_general(a, b, (((a_dim,), (b_dim,)), ((), ())), preferred_element_type=F32)


def layer_kernel(
    dims, x_ref, rate_ref, decay_ref, fast_rate_ref, wqkv_hbm, wout_hbm, fast_hbm, mom_hbm,
    handed_ref, next_hbm,
    wqkv, wout, fast, mom, moved, columns, rates, rate_in, part, outer_in, cross_in, final,
    qpart, qouter_in, qcross_in, qfinal, grad, updated, mixed, half_out, half_in, sent, hand,
    load_sem, x_send, x_recv, fwd_send, fwd_recv, rate_send, rate_recv,
    s_send, o_recv, c_recv, f_send, f_recv, qs_send, qo_recv, qc_recv, qf_send, qf_recv,
    next_sem, half_send, half_recv, hand_send, hand_recv,
):
    sections, n, heads, fin, hid = dims
    rows = x_ref.shape[0]
    width = columns.shape[3]
    half = rows // 2
    all_rows = rows * n
    local = heads * fin
    per_block = rows // CHUNK
    chunks = n * per_block
    qchunks = all_rows // QUERY_CHUNK
    sec, me, core = lax.axis_index("section"), lax.axis_index("tok"), lax.axis_index("head")
    mate = 1 - core
    right = me // (n // 2)
    inner, outer = me + 1 - 2 * right, me - 1 + 2 * right
    is_end = (me == 0) | (me == n - 1)
    is_mid = (me == n // 2 - 1) | (me == n // 2)
    share = n // 2
    next_sec, last_sec = lax.rem(sec + 1, sections), lax.rem(sec + sections - 1, sections)
    peers = [lax.rem(me + step, n) for step in range(1, n)]

    loads = [
        pltpu.make_async_copy(src, dst, load_sem.at[i])
        for i, (src, dst) in enumerate(
            [(wqkv_hbm, wqkv), (fast_hbm, fast), (mom_hbm, mom), (wout_hbm, wout)]
        )
    ]
    for load in loads:
        load.start()

    barrier = pltpu.get_barrier_semaphore()

    def greet(device):
        pl.semaphore_signal(barrier, inc=1, device_id=device, device_id_type=MESH)

    for peer in peers:
        greet((sec, peer, core))
    greet((sec, me, mate))
    for j in range(share):
        greet((next_sec, core * share + j, me // share))
        greet((last_sec, core * share + j, me // share))
    pl.semaphore_wait(barrier, n + 2 * share)

    def remote(src, dst, send, recv, device):
        return pltpu.make_async_remote_copy(
            src_ref=src, dst_ref=dst, send_sem=send, recv_sem=recv,
            device_id=device, device_id_type=MESH,
        )

    def x_copy(peer):
        start = pl.multiple_of(peer * width, 128)
        return remote(
            x_ref.at[pl.ds(core * half, half), pl.ds(start, width)], columns.at[me, core],
            x_send.at[peer], x_recv.at[me], (sec, peer, core),
        )

    def x_from(source):
        return remote(
            columns.at[source, core], columns.at[source, core],
            x_send.at[source], x_recv.at[source], (sec, source, core),
        )

    def x_forward(source):
        return remote(
            columns.at[source, core], columns.at[source, core],
            fwd_send.at[source], fwd_recv.at[source], (sec, me, mate),
        )

    def x_forwarded(source):
        return remote(
            columns.at[source, mate], columns.at[source, mate],
            fwd_send.at[source], fwd_recv.at[source], (sec, me, mate),
        )

    def rate_copy(peer, slot):
        return remote(
            rate_ref, rate_in.at[slot], rate_send.at[peer], rate_recv.at[slot], (sec, peer, core)
        )

    for peer in peers:
        x_copy(peer).start()
        rate_copy(peer, me).start()
    own = x_ref[:, pl.ds(pl.multiple_of(me * width, 128), width)]
    columns[me] = own.reshape(2, half, width)

    def normed(values, epsilon):
        return values * lax.rsqrt(jnp.mean(values * values, axis=-1, keepdims=True) + epsilon)

    def stages(part, outer_in, cross_in, final, s_send, o_recv, c_recv, f_send, f_recv, finish):
        def to_outer_in(c):
            return remote(part.at[c], outer_in.at[c], s_send.at[c], o_recv.at[c], (sec, inner, core))

        def to_cross_in(c):
            return remote(part.at[c], cross_in.at[c], s_send.at[c], c_recv.at[c], (sec, inner, core))

        def outward(c):
            return remote(final.at[c], final.at[c], f_send.at[c], f_recv.at[c], (sec, outer, core))

        def gather(c):
            @pl.when(jnp.logical_not(is_end))
            def _():
                to_outer_in(c).wait_recv()
                part[c] = (part[c].astype(F32) + outer_in[c].astype(F32)).astype(BF16)

            @pl.when(is_mid)
            def _():
                to_cross_in(c).start()

            @pl.when(jnp.logical_not(is_mid))
            def _():
                to_outer_in(c).start()

        def spread(c):
            @pl.when(is_mid)
            def _():
                to_cross_in(c).wait_recv()
                finish(c, part[c].astype(F32) + cross_in[c].astype(F32))

            @pl.when(jnp.logical_not(is_mid))
            def _():
                outward(c).wait_recv()

            @pl.when(jnp.logical_not(is_end))
            def _():
                outward(c).start()

        def drain(c):
            to_outer_in(c).wait_send()

            @pl.when(jnp.logical_not(is_end))
            def _():
                outward(c).wait_send()

        return gather, spread, drain

    def finish_kv(c, total):
        block, row = c // per_block, (c % per_block) * CHUNK
        for h in range(heads):
            lanes = slice(h * fin, (h + 1) * fin)
            final[c, :, lanes] = normed(total[:, lanes], 1e-06).astype(BF16)
            value = total[:, local + h * fin : local + (h + 1) * fin].astype(BF16).astype(F32)
            rate = rates[h, block, pl.ds(pl.multiple_of(row, CHUNK), CHUNK), :][:, :1]
            final[c, :, local + h * fin : local + (h + 1) * fin] = (-(rate * value)).astype(BF16)

    def finish_q(c, total):
        for h in range(heads):
            lanes = slice(h * fin, (h + 1) * fin)
            qfinal[c, :, lanes] = normed(total[:, lanes], 1e-06).astype(BF16)

    gather, spread, drain = stages(
        part, outer_in, cross_in, final, s_send, o_recv, c_recv, f_send, f_recv, finish_kv
    )
    qgather, qspread, qdrain = stages(
        qpart, qouter_in, qcross_in, qfinal, qs_send, qo_recv, qc_recv, qf_send, qf_recv, finish_q
    )

    for block in range(n):
        @pl.when(me != block)
        def _():
            x_from(block).wait_recv()
            x_forward(block).start()
            rate_copy(block, block).wait_recv()
            x_forwarded(block).wait_recv()
            for h in range(heads):
                line = rate_in[block, h : h + 1, :]
                rates[h, block] = jnp.transpose(jnp.broadcast_to(line, (rows, rows)))

        @pl.when(me == block)
        def _():
            for h in range(heads):
                line = rate_ref[h : h + 1, :]
                rates[h, block] = jnp.transpose(jnp.broadcast_to(line, (rows, rows)))

        if block == 0:
            loads[0].wait()
        tile = columns[block].reshape(rows, width)
        for j in range(2):
            made = dot(tile, wqkv[j + 1]).astype(BF16).reshape(per_block, CHUNK, local)
            part[block * per_block : (block + 1) * per_block, :, j * local : (j + 1) * local] = made

        @pl.loop(block * per_block, (block + 1) * per_block)
        def _(c):
            gather(c)

            @pl.when(jnp.logical_not(is_end) & (c >= LAG))
            def _():
                spread(c - LAG)

    tile = columns[...].reshape(all_rows, width)
    qpart[...] = dot(tile, wqkv[0]).astype(BF16).reshape(qchunks, QUERY_CHUNK, local)

    @pl.when(is_end)
    def _():
        @pl.loop(0, qchunks)
        def _(c):
            qgather(c)

        @pl.loop(0, chunks)
        def _(c):
            spread(c)

    @pl.when(jnp.logical_not(is_end))
    def _():
        @pl.loop(chunks - LAG, chunks)
        def _(c):
            spread(c)

    def query_step(c):
        @pl.when(jnp.logical_not(is_end) & (c < qchunks))
        def _():
            qgather(c)

        @pl.when(jnp.logical_not(is_end) & (c >= 2) & (c < qchunks + 2))
        def _():
            qspread(c - 2)

    loads[1].wait()
    loads[2].wait()

    def store_next(m):
        return pltpu.make_async_copy(updated.at[m], next_hbm.at[m], next_sem.at[m])

    @pl.loop(0, heads)
    def _(h):
        lanes = pl.ds(pl.multiple_of(h * fin, 128), fin)
        err_lanes = pl.ds(pl.multiple_of(local + h * fin, 128), fin)
        keys = final[:, :, lanes].reshape(all_rows, fin)
        errors = final[:, :, err_lanes].reshape(all_rows, fin)
        gate = dot(keys, fast[h * 3])
        squash = jax.nn.sigmoid(gate)
        up = dot(keys, fast[h * 3 + 1])
        hidden = (gate * squash * up).astype(BF16)
        back = dot(errors, fast[h * 3 + 2])
        grad_gate = (back * up * squash * (1.0 + gate * (1.0 - squash))).astype(BF16)
        grad_up = (back * gate * squash).astype(BF16)
        grad[0] = dot(keys, grad_gate, 0, 0)
        grad[1] = dot(keys, grad_up, 0, 0)
        grad[2] = dot(errors, hidden, 0, 0)

        @pl.loop(0, 3)
        def _(j):
            m = h * 3 + j
            moment = decay_ref[h] * mom[m].astype(F32) + grad[j]
            size = jnp.sqrt(jnp.sum(moment * moment))
            moved[...] = (moment / (size + 1e-06)).astype(BF16)
            for _ in range(NS_ITERS):
                it = moved[...]
                gram = dot(it, it, 0, 0).astype(BF16)
                cubic = dot(it, gram)
                quintic = dot(cubic.astype(BF16), gram)
                moved[...] = (
                    coef_linear * it.astype(F32) + coef_cubic * cubic + coef_quintic * quintic
                ).astype(BF16)
            updated[m] = (
                fast[m].astype(F32) - fast_rate_ref[h] * moved[...].astype(F32)
            ).astype(BF16)
            store_next(m).start()
            query_step(m)

    @pl.loop(heads * 3, qchunks + 2)
    def _(c):
        query_step(c)

    @pl.when(is_end)
    def _():
        @pl.loop(0, qchunks)
        def _(c):
            qspread(c)

    @pl.loop(0, heads)
    def _(h):
        lanes = pl.ds(pl.multiple_of(h * fin, 128), fin)
        queries = qfinal[:, :, lanes].reshape(all_rows, fin)
        gate = dot(queries, updated[h * 3])
        up = dot(queries, updated[h * 3 + 1])
        hidden = (gate * jax.nn.sigmoid(gate) * up).astype(BF16)
        output = dot(hidden, updated[h * 3 + 2], 1, 1)
        mixed[:, lanes] = normed(output, 1e-05).astype(BF16)

    loads[3].wait()
    span = all_rows // 2
    mine = pl.ds(pl.multiple_of(core * span, 128), span)
    theirs = pl.ds(pl.multiple_of(mate * span, 128), span)
    half_out[...] = dot(mixed[theirs, :], wout[...]).astype(BF16)
    swap = remote(half_out, half_in, half_send, half_recv, (sec, me, mate))
    swap.start()
    summed = dot(mixed[mine, :], wout[...])
    residual = columns[pl.ds(core * share, share)].reshape(span, width).astype(F32)
    swap.wait()
    sent[...] = (residual + (summed + half_in[...].astype(F32))).astype(BF16).reshape(
        share, rows, width
    )

    def hand_over(j, slot):
        return remote(
            sent.at[j], hand.at[slot], hand_send.at[j], hand_recv.at[slot],
            (next_sec, core * share + j, me // share),
        )

    for j in range(share):
        hand_over(j, lax.rem(me, share)).start()
    for peer in peers:
        x_copy(peer).wait_send()
        rate_copy(peer, me).wait_send()
        x_forward(peer).wait_send()

    @pl.loop(0, chunks)
    def _(c):
        drain(c)

    @pl.loop(0, qchunks)
    def _(c):
        qdrain(c)

    for m in range(heads * 3):
        store_next(m).wait()
    for j in range(share):
        hand_over(j, j).wait_recv()
        handed_ref[:, j * width : (j + 1) * width] = hand[j]
    for j in range(share):
        hand_over(j, j).wait_send()


def fused_shards(
    group_in, w_qkv, w_out, step_sizes, fast_weights, momentum, momentum_decay, fast_rate
):
    sections, n = lax.axis_size("section"), lax.axis_size("tok")
    tokens = group_in[0]
    rows = tokens.shape[0]
    heads, fin, hid = fast_weights.shape[1], fast_weights.shape[3], fast_weights.shape[4]
    local, width = heads * fin, w_qkv.shape[2]
    all_rows, share = rows * n, n // 2
    chunks, qchunks = all_rows // CHUNK, all_rows // QUERY_CHUNK
    matrices = heads * 3
    rate_lines = jnp.pad(step_sizes[0].T, ((0, 8 - heads), (0, 0)))
    vmem = pl.BlockSpec(memory_space=pltpu.VMEM)
    smem = pl.BlockSpec(memory_space=pltpu.SMEM)
    anywhere = pl.BlockSpec(memory_space=pl.ANY)
    dma = pltpu.SemaphoreType.DMA
    handed, updated = pl.pallas_call(
        functools.partial(layer_kernel, (sections, n, heads, fin, hid)),
        out_shape=(
            jax.ShapeDtypeStruct((rows, share * width), BF16),
            jax.ShapeDtypeStruct((matrices, fin, hid), BF16),
        ),
        in_specs=[vmem, vmem, smem, smem, anywhere, anywhere, anywhere, anywhere],
        out_specs=(vmem, anywhere),
        scratch_shapes=[
            pltpu.VMEM(w_qkv.shape[1:], BF16),
            pltpu.VMEM(w_out.shape[1:], BF16),
            pltpu.VMEM((matrices, fin, hid), BF16),
            pltpu.VMEM((matrices, fin, hid), BF16),
            pltpu.VMEM((fin, hid), BF16),
            pltpu.VMEM((n, 2, rows // 2, width), BF16),
            pltpu.VMEM((heads, n, rows, rows), F32),
            pltpu.VMEM((n, 8, rows), F32),
            pltpu.VMEM((chunks, CHUNK, 2 * local), BF16),
            pltpu.VMEM((chunks, CHUNK, 2 * local), BF16),
            pltpu.VMEM((chunks, CHUNK, 2 * local), BF16),
            pltpu.VMEM((chunks, CHUNK, 2 * local), BF16),
            pltpu.VMEM((qchunks, QUERY_CHUNK, local), BF16),
            pltpu.VMEM((qchunks, QUERY_CHUNK, local), BF16),
            pltpu.VMEM((qchunks, QUERY_CHUNK, local), BF16),
            pltpu.VMEM((qchunks, QUERY_CHUNK, local), BF16),
            pltpu.VMEM((3, fin, hid), F32),
            pltpu.VMEM((matrices, fin, hid), BF16),
            pltpu.VMEM((all_rows, local), BF16),
            pltpu.VMEM((all_rows // 2, width), BF16),
            pltpu.VMEM((all_rows // 2, width), BF16),
            pltpu.VMEM((share, rows, width), BF16),
            pltpu.VMEM((share, rows, width), BF16),
            dma((4,)),
            dma((n,)), dma((n,)), dma((n,)), dma((n,)), dma((n,)), dma((n,)),
            dma((chunks,)), dma((chunks,)), dma((chunks,)), dma((chunks,)), dma((chunks,)),
            dma((qchunks,)), dma((qchunks,)), dma((qchunks,)), dma((qchunks,)), dma((qchunks,)),
            dma((matrices,)), dma(()), dma(()), dma((share,)), dma((share,)),
        ],
        compiler_params=pltpu.CompilerParams(
            collective_id=0, has_side_effects=True, vmem_limit_bytes=60 << 20
        ),
    )(
        tokens, rate_lines, momentum_decay[0], fast_rate[0], w_qkv[0], w_out[0],
        fast_weights[0].reshape(matrices, fin, hid), momentum[0].reshape(matrices, fin, hid),
    )
    return (handed[None], updated.reshape(fast_weights.shape))


def shards(group_in, w_qkv, w_out, *rest):
    n, cores = lax.axis_size("tok"), lax.axis_size("head")
    rows, width, local = group_in.shape[1], w_qkv.shape[2], w_qkv.shape[3]
    held = 2 * (24 * rows * n * local + 12 * rows * n * width + 4 * w_qkv[0].size)
    fits = (
        held < 44 << 20
        and cores == 2
        and n % 2 == 0
        and n >= 4
        and rows == 128
        and width % 128 == 0
        and w_out.shape[2] == width
        and lax.axis_size("section") > 2
    )
    return (fused_shards if fits else plain_shards)(group_in, w_qkv, w_out, *rest)


def solution(mesh):
    placed = (
        P("section", "tok", None),
        P("section", None, "tok", "head"),
        P("section", "head", "tok"),
        P("section", "tok", "head"),
        P("section", "head", None, None, None),
        P("section", "head", None, None, None),
        P("section", "head"),
        P("section", "head"),
    )
    return jax.shard_map(
        shards,
        mesh=mesh,
        in_specs=placed,
        out_specs=(P("section", "tok", "head"), P("section", "head", None, None, None)),
        check_vma=False,
    )
```

```python
import functools

import jax
import jax.numpy as jnp
from jax import lax
from jax.experimental import pallas as pl
from jax.experimental.pallas import tpu as pltpu
from jax.sharding import PartitionSpec as P

NS_ITERS = 2


coef_linear = 3.4445
coef_cubic = -4.775
coef_quintic = 2.0315


def passed_along(value, axis, steps):
    count = lax.axis_size(axis)
    pairs = [(source, (source + steps) % count) for source in range(count)]
    return lax.ppermute(value, axis, pairs)


def rms_rows(values_in, epsilon):
    return values_in * lax.rsqrt(jnp.mean(values_in * values_in, axis=-1, keepdims=True) + epsilon)


def fast_grads(key_rows, value_rows, step_rates, weights):
    gate_pre = jnp.einsum(
        "thi,hij->thj", key_rows, weights[:, 0], preferred_element_type=jnp.float32
    )
    up_pre = jnp.einsum("thi,hij->thj", key_rows, weights[:, 1], preferred_element_type=jnp.float32)
    squash = jax.nn.sigmoid(gate_pre)
    hidden = (gate_pre * squash * up_pre).astype(jnp.bfloat16)
    errors = (-(step_rates[:, :, None] * value_rows.astype(jnp.float32))).astype(jnp.bfloat16)
    back_hidden = jnp.einsum(
        "thi,hij->thj", errors, weights[:, 2], preferred_element_type=jnp.float32
    )
    grad_gate = (back_hidden * up_pre * squash * (1.0 + gate_pre * (1.0 - squash))).astype(
        jnp.bfloat16
    )
    grad_up = (back_hidden * gate_pre * squash).astype(jnp.bfloat16)
    grad_first = jnp.einsum("thi,thj->hij", key_rows, grad_gate, preferred_element_type=jnp.float32)
    grad_third = jnp.einsum("thi,thj->hij", key_rows, grad_up, preferred_element_type=jnp.float32)
    grad_second = jnp.einsum("thi,thj->hij", errors, hidden, preferred_element_type=jnp.float32)
    return jnp.stack([grad_first, grad_third, grad_second], axis=1)


def newton_step(rows_in, gathered):
    gram_matrix = jnp.einsum(
        "mij,mik->mjk", gathered, gathered, preferred_element_type=jnp.float32
    ).astype(jnp.bfloat16)
    cubic_term = jnp.einsum(
        "mij,mjk->mik", rows_in, gram_matrix, preferred_element_type=jnp.float32
    )
    quintic_term = jnp.einsum(
        "mij,mjk->mik",
        cubic_term.astype(jnp.bfloat16),
        gram_matrix,
        preferred_element_type=jnp.float32,
    )
    return (
        coef_linear * rows_in.astype(jnp.float32)
        + coef_cubic * cubic_term
        + coef_quintic * quintic_term
    ).astype(jnp.bfloat16)


def apply_fast(queries, updated):
    gate_pre = jnp.einsum(
        "thi,hij->thj", queries, updated[:, 0], preferred_element_type=jnp.float32
    )
    up_pre = jnp.einsum("thi,hij->thj", queries, updated[:, 1], preferred_element_type=jnp.float32)
    hidden = (jax.nn.silu(gate_pre) * up_pre).astype(jnp.bfloat16)
    output = jnp.einsum("thj,hij->thi", hidden, updated[:, 2], preferred_element_type=jnp.float32)
    return rms_rows(output, 1e-05).astype(jnp.bfloat16)


def plain_shards(group_in, w_qkv, w_out, step_sizes, fast_weights, momentum, momentum_decay, fast_rate):
    tokens = group_in[0]
    tok_rows = tokens.shape[0]
    local_heads = fast_weights.shape[1]
    fan_width = fast_weights.shape[3]
    hid_width = fast_weights.shape[4]
    half_width = w_qkv.shape[3]
    columns = lax.all_to_all(tokens, "tok", split_axis=1, concat_axis=0, tiled=True)
    all_rows = columns.shape[0]
    rates = lax.all_gather(step_sizes[0], "tok", axis=0, tiled=True)
    partial_kv = jnp.einsum(
        "td,jde->jte", columns, w_qkv[0, 1:], preferred_element_type=jnp.float32
    ).astype(jnp.bfloat16)
    partial_q = jnp.dot(columns, w_qkv[0, 0], preferred_element_type=jnp.float32).astype(
        jnp.bfloat16
    )
    summed_kv = lax.psum(partial_kv, "tok").astype(jnp.float32)
    summed_q = lax.psum(partial_q, "tok").astype(jnp.float32)
    shaped = summed_kv.reshape(2, all_rows, local_heads, fan_width)
    key_rows = rms_rows(shaped[0], 1e-06).astype(jnp.bfloat16)
    value_rows = shaped[1].astype(jnp.bfloat16)
    queries = rms_rows(summed_q.reshape(all_rows, local_heads, fan_width), 1e-06).astype(
        jnp.bfloat16
    )
    summed = fast_grads(key_rows, value_rows, rates, fast_weights[0])
    decay_rate = momentum_decay[0][:, None, None, None]
    moment = decay_rate * momentum[0].astype(jnp.float32) + summed
    norm_values = jnp.sqrt(jnp.sum(moment * moment, axis=(2, 3), keepdims=True))
    iterate = (moment / (norm_values + 1e-06)).astype(jnp.bfloat16)
    iterate = iterate.reshape(local_heads * 3, fan_width, hid_width)
    for number in range(NS_ITERS):
        iterate = newton_step(iterate, iterate)
    iterate = iterate.reshape(local_heads, 3, fan_width, hid_width)
    updated = (
        fast_weights[0].astype(jnp.float32)
        - fast_rate[0][:, None, None, None] * iterate.astype(jnp.float32)
    ).astype(jnp.bfloat16)
    mixed_heads = apply_fast(queries, updated).reshape(all_rows, half_width)
    partial_out = jnp.dot(mixed_heads, w_out[0], preferred_element_type=jnp.float32)
    own_rows = lax.all_to_all(
        partial_out.astype(jnp.bfloat16), "tok", split_axis=0, concat_axis=1, tiled=True
    )
    summed_out = lax.psum_scatter(own_rows, "head", scatter_dimension=1, tiled=True).astype(
        jnp.float32
    )
    share_width = summed_out.shape[1]
    own_tokens = lax.dynamic_slice_in_dim(
        tokens, lax.axis_index("head") * share_width, share_width, 1
    )
    layer_out = (own_tokens.astype(jnp.float32) + summed_out).astype(jnp.bfloat16)
    handed = passed_along(layer_out[None], "section", 1)
    return (handed, updated[None])


MESH = pl.DeviceIdType.MESH
F32 = jnp.float32
BF16 = jnp.bfloat16
CHUNK = 32
QUERY_CHUNK = 64
LAG = 3


def dot(a, b, a_dim=1, b_dim=0):
    return lax.dot_general(a, b, (((a_dim,), (b_dim,)), ((), ())), preferred_element_type=F32)


def layer_kernel(
    dims, x_ref, rate_ref, decay_ref, fast_rate_ref, wqkv_hbm, wout_hbm, fast_hbm, mom_hbm,
    handed_ref, next_hbm,
    wqkv, wout, fast, mom, moved, columns, rates, rate_in, part, outer_in, cross_in, final,
    qpart, qouter_in, qcross_in, qfinal, grad, updated, mixed, half_out, half_in, sent, hand,
    load_sem, x_send, x_recv, fwd_send, fwd_recv, rate_send, rate_recv,
    s_send, o_recv, c_recv, f_send, f_recv, qs_send, qo_recv, qc_recv, qf_send, qf_recv,
    next_sem, half_send, half_recv, hand_send, hand_recv,
):
    sections, n, heads, fin, hid = dims
    rows = x_ref.shape[0]
    width = columns.shape[3]
    half = rows // 2
    all_rows = rows * n
    local = heads * fin
    per_block = rows // CHUNK
    chunks = n * per_block
    qchunks = all_rows // QUERY_CHUNK
    sec, me, core = lax.axis_index("section"), lax.axis_index("tok"), lax.axis_index("head")
    mate = 1 - core
    right = me // (n // 2)
    inner, outer = me + 1 - 2 * right, me - 1 + 2 * right
    is_end = (me == 0) | (me == n - 1)
    is_mid = (me == n // 2 - 1) | (me == n // 2)
    share = n // 2
    next_sec, last_sec = lax.rem(sec + 1, sections), lax.rem(sec + sections - 1, sections)
    peers = [lax.rem(me + step, n) for step in range(1, n)]

    loads = [
        pltpu.make_async_copy(src, dst, load_sem.at[i])
        for i, (src, dst) in enumerate(
            [(wqkv_hbm, wqkv), (fast_hbm, fast), (mom_hbm, mom), (wout_hbm, wout)]
        )
    ]
    loads[0].start()

    barrier = pltpu.get_barrier_semaphore()

    def greet(device):
        pl.semaphore_signal(barrier, inc=1, device_id=device, device_id_type=MESH)

    for peer in peers:
        greet((sec, peer, core))
    greet((sec, me, mate))
    for j in range(share):
        greet((next_sec, core * share + j, me // share))
        greet((last_sec, core * share + j, me // share))
    pl.semaphore_wait(barrier, n + 2 * share)

    def remote(src, dst, send, recv, device):
        return pltpu.make_async_remote_copy(
            src_ref=src, dst_ref=dst, send_sem=send, recv_sem=recv,
            device_id=device, device_id_type=MESH,
        )

    def x_copy(peer):
        start = pl.multiple_of(peer * width, 128)
        return remote(
            x_ref.at[pl.ds(core * half, half), pl.ds(start, width)], columns.at[me, core],
            x_send.at[peer], x_recv.at[me], (sec, peer, core),
        )

    def x_from(source):
        return remote(
            columns.at[source, core], columns.at[source, core],
            x_send.at[source], x_recv.at[source], (sec, source, core),
        )

    def x_forward(source):
        return remote(
            columns.at[source, core], columns.at[source, core],
            fwd_send.at[source], fwd_recv.at[source], (sec, me, mate),
        )

    def x_forwarded(source):
        return remote(
            columns.at[source, mate], columns.at[source, mate],
            fwd_send.at[source], fwd_recv.at[source], (sec, me, mate),
        )

    def rate_copy(peer, slot):
        return remote(
            rate_ref, rate_in.at[slot], rate_send.at[peer], rate_recv.at[slot], (sec, peer, core)
        )

    for peer in peers:
        x_copy(peer).start()
        rate_copy(peer, me).start()
    own = x_ref[:, pl.ds(pl.multiple_of(me * width, 128), width)]
    columns[me] = own.reshape(2, half, width)

    def normed(values, epsilon):
        return values * lax.rsqrt(jnp.mean(values * values, axis=-1, keepdims=True) + epsilon)

    def stages(part, outer_in, cross_in, final, s_send, o_recv, c_recv, f_send, f_recv, finish):
        def to_outer_in(c):
            return remote(part.at[c], outer_in.at[c], s_send.at[c], o_recv.at[c], (sec, inner, core))

        def to_cross_in(c):
            return remote(part.at[c], cross_in.at[c], s_send.at[c], c_recv.at[c], (sec, inner, core))

        def outward(c):
            return remote(final.at[c], final.at[c], f_send.at[c], f_recv.at[c], (sec, outer, core))

        def gather(c):
            @pl.when(jnp.logical_not(is_end))
            def _():
                to_outer_in(c).wait_recv()
                part[c] = (part[c].astype(F32) + outer_in[c].astype(F32)).astype(BF16)

            @pl.when(is_mid)
            def _():
                to_cross_in(c).start()

            @pl.when(jnp.logical_not(is_mid))
            def _():
                to_outer_in(c).start()

        def spread(c):
            @pl.when(is_mid)
            def _():
                to_cross_in(c).wait_recv()
                finish(c, part[c].astype(F32) + cross_in[c].astype(F32))

            @pl.when(jnp.logical_not(is_mid))
            def _():
                outward(c).wait_recv()

            @pl.when(jnp.logical_not(is_end))
            def _():
                outward(c).start()

        def drain(c):
            to_outer_in(c).wait_send()

            @pl.when(jnp.logical_not(is_end))
            def _():
                outward(c).wait_send()

        return gather, spread, drain

    def finish_kv(c, total):
        block, row = c // per_block, (c % per_block) * CHUNK
        for h in range(heads):
            lanes = slice(h * fin, (h + 1) * fin)
            final[c, :, lanes] = normed(total[:, lanes], 1e-06).astype(BF16)
            value = total[:, local + h * fin : local + (h + 1) * fin].astype(BF16).astype(F32)
            rate = rates[h, block, pl.ds(pl.multiple_of(row, CHUNK), CHUNK), :][:, :1]
            final[c, :, local + h * fin : local + (h + 1) * fin] = (-(rate * value)).astype(BF16)

    def finish_q(c, total):
        for h in range(heads):
            lanes = slice(h * fin, (h + 1) * fin)
            qfinal[c, :, lanes] = normed(total[:, lanes], 1e-06).astype(BF16)

    gather, spread, drain = stages(
        part, outer_in, cross_in, final, s_send, o_recv, c_recv, f_send, f_recv, finish_kv
    )
    qgather, qspread, qdrain = stages(
        qpart, qouter_in, qcross_in, qfinal, qs_send, qo_recv, qc_recv, qf_send, qf_recv, finish_q
    )

    for block in range(n):
        @pl.when(me != block)
        def _():
            x_from(block).wait_recv()
            x_forward(block).start()
            rate_copy(block, block).wait_recv()
            x_forwarded(block).wait_recv()
            for h in range(heads):
                line = rate_in[block, h : h + 1, :]
                rates[h, block] = jnp.transpose(jnp.broadcast_to(line, (rows, rows)))

        @pl.when(me == block)
        def _():
            for h in range(heads):
                line = rate_ref[h : h + 1, :]
                rates[h, block] = jnp.transpose(jnp.broadcast_to(line, (rows, rows)))

        if block == 0:
            loads[0].wait()
            for load in loads[1:]:
                load.start()
        tile = columns[block].reshape(rows, width)
        for j in range(2):
            made = dot(tile, wqkv[j + 1]).astype(BF16).reshape(per_block, CHUNK, local)
            part[block * per_block : (block + 1) * per_block, :, j * local : (j + 1) * local] = made

        @pl.loop(block * per_block, (block + 1) * per_block)
        def _(c):
            gather(c)

            @pl.when(jnp.logical_not(is_end) & (c >= LAG))
            def _():
                spread(c - LAG)

        made = dot(columns[block].reshape(rows, width), wqkv[0]).astype(BF16)
        per_query = rows // QUERY_CHUNK
        qpart[block * per_query : (block + 1) * per_query] = made.reshape(
            per_query, QUERY_CHUNK, local
        )

    @pl.when(is_end)
    def _():
        @pl.loop(0, qchunks)
        def _(c):
            qgather(c)

        @pl.loop(0, chunks)
        def _(c):
            spread(c)

    @pl.when(jnp.logical_not(is_end))
    def _():
        @pl.loop(chunks - LAG, chunks)
        def _(c):
            spread(c)

    def query_step(c):
        @pl.when(jnp.logical_not(is_end) & (c < qchunks))
        def _():
            qgather(c)

        @pl.when(jnp.logical_not(is_end) & (c >= LAG) & (c < qchunks + LAG))
        def _():
            qspread(c - LAG)

    loads[1].wait()
    loads[2].wait()

    def store_next(m):
        return pltpu.make_async_copy(updated.at[m], next_hbm.at[m], next_sem.at[m])

    @pl.loop(0, heads)
    def _(h):
        lanes = pl.ds(pl.multiple_of(h * fin, 128), fin)
        err_lanes = pl.ds(pl.multiple_of(local + h * fin, 128), fin)
        keys = final[:, :, lanes].reshape(all_rows, fin)
        errors = final[:, :, err_lanes].reshape(all_rows, fin)
        gate = dot(keys, fast[h * 3])
        squash = jax.nn.sigmoid(gate)
        up = dot(keys, fast[h * 3 + 1])
        hidden = (gate * squash * up).astype(BF16)
        back = dot(errors, fast[h * 3 + 2])
        grad_gate = (back * up * squash * (1.0 + gate * (1.0 - squash))).astype(BF16)
        grad_up = (back * gate * squash).astype(BF16)
        grad[0] = dot(keys, grad_gate, 0, 0)
        grad[1] = dot(keys, grad_up, 0, 0)
        grad[2] = dot(errors, hidden, 0, 0)

        @pl.loop(0, 3)
        def _(j):
            m = h * 3 + j
            moment = decay_ref[h] * mom[m].astype(F32) + grad[j]
            size = jnp.sqrt(jnp.sum(moment * moment))
            moved[...] = (moment / (size + 1e-06)).astype(BF16)
            for _ in range(NS_ITERS):
                it = moved[...]
                gram = dot(it, it, 0, 0).astype(BF16)
                cubic = dot(it, gram)
                quintic = dot(cubic.astype(BF16), gram)
                moved[...] = (
                    coef_linear * it.astype(F32) + coef_cubic * cubic + coef_quintic * quintic
                ).astype(BF16)
            updated[m] = (
                fast[m].astype(F32) - fast_rate_ref[h] * moved[...].astype(F32)
            ).astype(BF16)
            store_next(m).start()
            query_step(2 * m)
            query_step(2 * m + 1)

    @pl.loop(heads * 6, max(heads * 6, qchunks + LAG))
    def _(c):
        query_step(c)

    @pl.when(is_end)
    def _():
        @pl.loop(0, qchunks)
        def _(c):
            qspread(c)

    @pl.loop(0, heads)
    def _(h):
        lanes = pl.ds(pl.multiple_of(h * fin, 128), fin)
        queries = qfinal[:, :, lanes].reshape(all_rows, fin)
        gate = dot(queries, updated[h * 3])
        up = dot(queries, updated[h * 3 + 1])
        hidden = (gate * jax.nn.sigmoid(gate) * up).astype(BF16)
        output = dot(hidden, updated[h * 3 + 2], 1, 1)
        mixed[:, lanes] = normed(output, 1e-05).astype(BF16)

    loads[3].wait()
    span = all_rows // 2
    mine = pl.ds(pl.multiple_of(core * span, 128), span)
    theirs = pl.ds(pl.multiple_of(mate * span, 128), span)
    half_out[...] = dot(mixed[theirs, :], wout[...]).astype(BF16)
    swap = remote(half_out, half_in, half_send, half_recv, (sec, me, mate))
    swap.start()
    summed = dot(mixed[mine, :], wout[...])
    residual = columns[pl.ds(core * share, share)].reshape(span, width).astype(F32)
    swap.wait()
    sent[...] = (residual + (summed + half_in[...].astype(F32))).astype(BF16).reshape(
        share, rows, width
    )

    def hand_over(j, slot):
        return remote(
            sent.at[j], hand.at[slot], hand_send.at[j], hand_recv.at[slot],
            (next_sec, core * share + j, me // share),
        )

    for j in range(share):
        hand_over(j, lax.rem(me, share)).start()
    for peer in peers:
        x_copy(peer).wait_send()
        rate_copy(peer, me).wait_send()
        x_forward(peer).wait_send()

    @pl.loop(0, chunks)
    def _(c):
        drain(c)

    @pl.loop(0, qchunks)
    def _(c):
        qdrain(c)

    for m in range(heads * 3):
        store_next(m).wait()
    for j in range(share):
        hand_over(j, j).wait_recv()
        handed_ref[:, j * width : (j + 1) * width] = hand[j]
    for j in range(share):
        hand_over(j, j).wait_send()


def fused_shards(
    group_in, w_qkv, w_out, step_sizes, fast_weights, momentum, momentum_decay, fast_rate
):
    sections, n = lax.axis_size("section"), lax.axis_size("tok")
    tokens = group_in[0]
    rows = tokens.shape[0]
    heads, fin, hid = fast_weights.shape[1], fast_weights.shape[3], fast_weights.shape[4]
    local, width = heads * fin, w_qkv.shape[2]
    all_rows, share = rows * n, n // 2
    chunks, qchunks = all_rows // CHUNK, all_rows // QUERY_CHUNK
    matrices = heads * 3
    rate_lines = jnp.pad(step_sizes[0].T, ((0, 8 - heads), (0, 0)))
    vmem = pl.BlockSpec(memory_space=pltpu.VMEM)
    smem = pl.BlockSpec(memory_space=pltpu.SMEM)
    anywhere = pl.BlockSpec(memory_space=pl.ANY)
    dma = pltpu.SemaphoreType.DMA
    handed, updated = pl.pallas_call(
        functools.partial(layer_kernel, (sections, n, heads, fin, hid)),
        out_shape=(
            jax.ShapeDtypeStruct((rows, share * width), BF16),
            jax.ShapeDtypeStruct((matrices, fin, hid), BF16),
        ),
        in_specs=[vmem, vmem, smem, smem, anywhere, anywhere, anywhere, anywhere],
        out_specs=(vmem, anywhere),
        scratch_shapes=[
            pltpu.VMEM(w_qkv.shape[1:], BF16),
            pltpu.VMEM(w_out.shape[1:], BF16),
            pltpu.VMEM((matrices, fin, hid), BF16),
            pltpu.VMEM((matrices, fin, hid), BF16),
            pltpu.VMEM((fin, hid), BF16),
            pltpu.VMEM((n, 2, rows // 2, width), BF16),
            pltpu.VMEM((heads, n, rows, rows), F32),
            pltpu.VMEM((n, 8, rows), F32),
            pltpu.VMEM((chunks, CHUNK, 2 * local), BF16),
            pltpu.VMEM((chunks, CHUNK, 2 * local), BF16),
            pltpu.VMEM((chunks, CHUNK, 2 * local), BF16),
            pltpu.VMEM((chunks, CHUNK, 2 * local), BF16),
            pltpu.VMEM((qchunks, QUERY_CHUNK, local), BF16),
            pltpu.VMEM((qchunks, QUERY_CHUNK, local), BF16),
            pltpu.VMEM((qchunks, QUERY_CHUNK, local), BF16),
            pltpu.VMEM((qchunks, QUERY_CHUNK, local), BF16),
            pltpu.VMEM((3, fin, hid), F32),
            pltpu.VMEM((matrices, fin, hid), BF16),
            pltpu.VMEM((all_rows, local), BF16),
            pltpu.VMEM((all_rows // 2, width), BF16),
            pltpu.VMEM((all_rows // 2, width), BF16),
            pltpu.VMEM((share, rows, width), BF16),
            pltpu.VMEM((share, rows, width), BF16),
            dma((4,)),
            dma((n,)), dma((n,)), dma((n,)), dma((n,)), dma((n,)), dma((n,)),
            dma((chunks,)), dma((chunks,)), dma((chunks,)), dma((chunks,)), dma((chunks,)),
            dma((qchunks,)), dma((qchunks,)), dma((qchunks,)), dma((qchunks,)), dma((qchunks,)),
            dma((matrices,)), dma(()), dma(()), dma((share,)), dma((share,)),
        ],
        compiler_params=pltpu.CompilerParams(
            collective_id=0, has_side_effects=True, vmem_limit_bytes=60 << 20
        ),
    )(
        tokens, rate_lines, momentum_decay[0], fast_rate[0], w_qkv[0], w_out[0],
        fast_weights[0].reshape(matrices, fin, hid), momentum[0].reshape(matrices, fin, hid),
    )
    return (handed[None], updated.reshape(fast_weights.shape))


def shards(group_in, w_qkv, w_out, *rest):
    n, cores = lax.axis_size("tok"), lax.axis_size("head")
    rows, width, local = group_in.shape[1], w_qkv.shape[2], w_qkv.shape[3]
    held = 2 * (24 * rows * n * local + 12 * rows * n * width + 4 * w_qkv[0].size)
    fits = (
        held < 44 << 20
        and cores == 2
        and n % 2 == 0
        and n >= 4
        and rows == 128
        and width % 128 == 0
        and w_out.shape[2] == width
        and lax.axis_size("section") > 2
    )
    return (fused_shards if fits else plain_shards)(group_in, w_qkv, w_out, *rest)


def solution(mesh):
    placed = (
        P("section", "tok", None),
        P("section", None, "tok", "head"),
        P("section", "head", "tok"),
        P("section", "tok", "head"),
        P("section", "head", None, None, None),
        P("section", "head", None, None, None),
        P("section", "head"),
        P("section", "head"),
    )
    return jax.shard_map(
        shards,
        mesh=mesh,
        in_specs=placed,
        out_specs=(P("section", "tok", "head"), P("section", "head", None, None, None)),
        check_vma=False,
    )
```
